256 devices in a mesh: lat: 64 (over x, y_lo, z), dp: 4 (over y_hi, core).
Axes of the slice: x: 4, y: 4 (y_hi: 2, y_lo: 2; y = y_hi * 2 + y_lo), z: 8, core: 2. Of those that a mesh axis runs over, the one named last changes fastest.
Arguments:
- inputs: bfloat16 [2048, 4096], P('dp', 'lat'), may hold values from -6 to 6
- dec_bias: bfloat16 [4096], P('lat'), may hold values from -3 to 3
- enc_weight: bfloat16 [4096, 16384], P(None, 'lat'), may hold values from -0.09375 to 0.09375
- enc_bias: float32 [16384], P('lat'), may hold values from -3 to 3
- dec_weight: bfloat16 [16384, 4096], P('lat'), may hold values from -0.046875 to 0.046875
- other_recon: float32 [2048, 4096], P('dp', 'lat'), may hold values from -6 to 6
- active_blocks: int32 [2048, 128], P('dp', 'lat'), may hold values 0 or 1
Outputs:
- error_full: float32 [2048, 4096], P('dp', 'lat')
- mse_loss: float32 [], replicated
- grad_dec: float32 [16384, 4096], P(('lat', 'dp'))
- grad_enc: float32 [4096, 16384], P(None, ('lat', 'dp'))
The draws below stay inside these ranges and needn't reach their ends.
All inputs are finite; a program needn't handle non-finite values. No bound on the sum of `active_blocks` on one device may be relied on, other than what follows from the above.
Results may differ from the reference program's by a relative error of at most 0.0033.
Values may be sent and summed in bfloat16 or wider, within the bound.
A program may use at most 128 MiB of HBM per device.

```python
import jax
import jax.numpy as jnp
from jax import lax

D = 4096
BLOCK = 128
LATENTS = 16384
NBLK = 128
ROWS = 2048


def place_ends(drawn, stream_key, least, top_value):
    place = [jax.random.randint(jax.random.fold_in(stream_key, axis), (), 0, length) for axis, length in enumerate(drawn.shape)]
    longest = drawn.shape.index(max(drawn.shape))
    next_to = place[:longest] + [(place[longest] + 1) % drawn.shape[longest]] + place[longest + 1:]
    return drawn.at[tuple(place)].set(least).at[tuple(next_to)].set(top_value)


def block_levels(own_key, shape, pieces, least, top_value):
    def one(dim, blocks):
        draws = jax.random.uniform(jax.random.fold_in(jax.random.fold_in(own_key, 6), dim), (blocks,), jnp.float32, least / len(pieces), top_value / len(pieces))
        return jnp.repeat(jnp.exp(draws), shape[dim] // blocks).reshape((-1,) + (1,) * (len(shape) - dim - 1))

    loudness = one(*pieces[0])
    for cut in pieces[1:]:
        loudness = loudness * one(*cut)
    return loudness


def gaussian(stream_key, shape, width, most, cuts=(), dtype=jnp.bfloat16):
    values = jax.random.normal(stream_key, shape, jnp.float32) * width
    if len(cuts) > 0:
        values = block_levels(stream_key, shape, cuts, -0.22, 0.18) * values
    return jnp.clip(values, min=-most, max=most).astype(dtype)


def setup_inputs(seed: int = 0) -> dict:
    key_list = jax.random.split(jax.random.key(seed), 8)
    inputs = gaussian(key_list[0], (ROWS, D), 1.0, 6.0, ((0, 4), (1, 64)))
    dec_bias = gaussian(key_list[1], (D,), 0.5, 3.0, ((0, 64),))
    enc_weight = gaussian(key_list[2], (D, LATENTS), D ** -0.5, 0.09375, ((1, 64),))
    enc_bias = gaussian(key_list[3], (LATENTS,), 0.5, 3.0, ((0, 64),), jnp.float32)
    dec_weight = gaussian(key_list[4], (LATENTS, D), LATENTS ** -0.5, 0.046875, ((0, 64),))
    other_recon = gaussian(key_list[5], (ROWS, D), 1.0, 6.0, ((0, 4), (1, 64)), jnp.float32)
    active_blocks = place_ends((jax.random.randint(key_list[6], (ROWS, NBLK), 0, 3) < 1).astype(jnp.int32), jax.random.fold_in(key_list[6], 1), 0, 1)
    return {"inputs": inputs, "dec_bias": dec_bias, "enc_weight": enc_weight, "enc_bias": enc_bias, "dec_weight": dec_weight, "other_recon": other_recon, "active_blocks": active_blocks}


def reference(inputs, dec_bias, enc_weight, enc_bias, dec_weight, other_recon, active_blocks):
    centered = (inputs.astype(jnp.float32) - dec_bias.astype(jnp.float32)[None, :]).astype(jnp.bfloat16)
    pre_act = jnp.dot(centered, enc_weight, preferred_element_type=jnp.float32) + enc_bias[None, :]
    block_gate = jnp.repeat(active_blocks.astype(jnp.float32), BLOCK, axis=1)
    positive = jnp.maximum(pre_act, 0.0)
    activations = (positive * positive * block_gate).astype(jnp.bfloat16)
    recon = jnp.dot(activations, dec_weight, preferred_element_type=jnp.float32) + other_recon + dec_bias.astype(jnp.float32)[None, :]
    error_full = recon - inputs.astype(jnp.float32)
    mse_loss = jnp.mean(error_full * error_full)
    error_bf = error_full.astype(jnp.bfloat16)
    grad_dec = lax.dot_general(activations, error_bf, (((0,), (0,)), ((), ())), preferred_element_type=jnp.float32)
    dact = lax.dot_general(error_bf, dec_weight, (((1,), (1,)), ((), ())), preferred_element_type=jnp.float32)
    dpre = (dact * 2.0 * positive * block_gate).astype(jnp.bfloat16)
    grad_enc = lax.dot_general(centered, dpre, (((0,), (0,)), ((), ())), preferred_element_type=jnp.float32)
    return (error_full, mse_loss, grad_dec, grad_enc)
```

```python
import functools

import jax
import jax.numpy as jnp
from jax import lax
from jax.experimental import pallas as pl
from jax.experimental.pallas import tpu as pltpu
from jax.sharding import PartitionSpec as P

MESH = pl.DeviceIdType.MESH
NX, NY, NZ = 4, 2, 8
NSLOT = NX * NY * NZ
BF16, F32 = jnp.bfloat16, jnp.float32


def place():
    lat = lax.axis_index("lat")
    return lax.div(lat, NY * NZ), lax.rem(lax.div(lat, NZ), NY), lax.rem(lat, NZ)


def slot_id(x, y, z):
    return (lax.rem(x + 2 * NX, NX) * NY + lax.rem(y + 2, NY)) * NZ + lax.rem(z + 2 * NZ, NZ)


def offset(k):
    half = lax.div(k + 1, 2)
    return jnp.where(lax.rem(k, 2) == 1, -half, half)


class Tree:
    def __init__(self, swap):
        self.swap = swap
        self.na, self.nb = (NZ, NX) if swap else (NX, NZ)
        self.x, self.y, self.z = place()

    def sid(self, a, b, j):
        if self.swap:
            return slot_id(self.x + b, self.y + j, self.z + a)
        return slot_id(self.x + a, self.y + j, self.z + b)

    def parity(self, j):
        return lax.rem(self.y + j, 2)

    def column(self, a, j):
        n = self.na
        me = self.z if self.swap else self.x
        return lax.rem(me + a + 2 * n, n) * 2 + self.parity(j)


def wait_for(ref, sem):
    pltpu.make_async_copy(ref, ref, sem).wait()


def gather_tree(buf, send_sem, recv_sem, swap):
    t = Tree(swap)
    na, nb, sid = t.na, t.nb, t.sid

    def send(s, a=0, b=0, j=0):
        pltpu.make_async_remote_copy(
            src_ref=buf.at[s],
            dst_ref=buf.at[s],
            send_sem=send_sem,
            recv_sem=recv_sem.at[s],
            device_id={"lat": sid(a, b, j)},
            device_id_type=MESH,
        ).start()

    def wait(s):
        wait_for(buf.at[s], recv_sem.at[s])

    own, other = sid(0, 0, 0), sid(0, 0, 1)
    send(own, j=1)
    for s in (own, other):
        if s is other:
            wait(other)
        send(s, a=1)
        send(s, a=-1)
        send(s, b=1)
        send(s, b=-1)
    for h in range(1, na // 2 + 1):
        for j in range(2):
            if h < na // 2:
                sm, sp = sid(-h, 0, j), sid(h, 0, j)
                wait(sm)
                if h + 1 < na // 2:
                    send(sm, a=1)
                send(sm, b=1)
                send(sm, b=-1)
                wait(sp)
                if h + 1 < na // 2:
                    send(sp, a=-1)
                send(sp, b=1)
                send(sp, b=-1)
                if h + 1 == na // 2:
                    pl.when(t.parity(j) == 0)(functools.partial(send, sm, a=1))
                    pl.when(t.parity(j) == 1)(functools.partial(send, sp, a=-1))
            else:
                s = sid(h, 0, j)
                wait(s)
                send(s, b=1)
                send(s, b=-1)

    def hop(h, c, carry):
        a, j = offset(lax.div(c, 2)), lax.rem(c, 2)
        if h == nb // 2:
            wait(sid(a, h, j))
            return carry
        sm, sp = sid(a, -h, j), sid(a, h, j)
        wait(sm)
        if h + 1 < nb // 2:
            send(sm, b=1)
        else:
            pl.when(t.parity(j) == 0)(functools.partial(send, sm, b=1))
        wait(sp)
        if h + 1 < nb // 2:
            send(sp, b=-1)
        else:
            pl.when(t.parity(j) == 1)(functools.partial(send, sp, b=-1))
        return carry

    for h in range(1, nb // 2 + 1):
        lax.fori_loop(0, 2 * na, functools.partial(hop, h), 0)
    sent = buf.at[pl.ds(0, NSLOT - 1)]
    wait_for(sent, send_sem)


def scatter_tree(part, r1, r2, a1, a2, y1, send_sem, r1_sem, r2_sem, a1_sem, a2_sem, y1_sem, swap):
    t = Tree(swap)
    na, nb, sid = t.na, t.nb, t.sid

    def send(s, dst, sem, a=0, b=0, j=0):
        pltpu.make_async_remote_copy(
            src_ref=part.at[s],
            dst_ref=dst,
            send_sem=send_sem,
            recv_sem=sem,
            device_id={"lat": sid(a, b, j)},
            device_id_type=MESH,
        ).start()

    def take(s, ref, sem):
        wait_for(ref, sem)
        part[s] += ref[...]

    def col(c):
        k = na - 1 - lax.div(c, 2)
        return offset(k), lax.rem(c, 2)

    far = nb // 2

    def first(c, carry):
        a, j = col(c)
        s = sid(a, far, j)
        pl.when(t.parity(j) == 0)(functools.partial(send, s, r1.at[s], r1_sem.at[s], b=-1))
        pl.when(t.parity(j) == 1)(functools.partial(send, s, r1.at[s], r1_sem.at[s], b=1))
        return carry

    def hop(h, c, carry):
        a, j = col(c)
        sm, sp = sid(a, -h, j), sid(a, h, j)
        if h == far - 1:
            pl.when(t.parity(j) == 0)(functools.partial(take, sm, r1.at[sm], r1_sem.at[sm]))
            pl.when(t.parity(j) == 1)(functools.partial(take, sp, r1.at[sp], r1_sem.at[sp]))
        else:
            take(sm, r1.at[sm], r1_sem.at[sm])
            take(sp, r1.at[sp], r1_sem.at[sp])
        send(sm, r1.at[sm], r1_sem.at[sm], b=-1)
        if h > 1:
            send(sp, r1.at[sp], r1_sem.at[sp], b=1)
        else:
            k = t.column(a, j)
            send(sp, r2.at[k], r2_sem.at[k], b=1)
        return carry

    lax.fori_loop(0, 2 * na, first, 0)
    for h in range(far - 1, 0, -1):
        lax.fori_loop(0, 2 * na, functools.partial(hop, h), 0)

    def own_b(a, j):
        s, k = sid(a, 0, j), t.column(a, j)
        take(s, r1.at[s], r1_sem.at[s])
        take(s, r2.at[k], r2_sem.at[k])
        return s, k

    fara = na // 2
    for j in range(2):
        s, k = own_b(fara, j)
        pl.when(t.parity(j) == 0)(functools.partial(send, s, a1.at[k], a1_sem.at[k], a=-1))
        pl.when(t.parity(j) == 1)(functools.partial(send, s, a1.at[k], a1_sem.at[k], a=1))
    for h in range(fara - 1, 0, -1):
        for j in range(2):
            sm, km = own_b(-h, j)
            sp, kp = own_b(h, j)
            if h == fara - 1:
                pl.when(t.parity(j) == 0)(functools.partial(take, sm, a1.at[km], a1_sem.at[km]))
                pl.when(t.parity(j) == 1)(functools.partial(take, sp, a1.at[kp], a1_sem.at[kp]))
            else:
                take(sm, a1.at[km], a1_sem.at[km])
                take(sp, a1.at[kp], a1_sem.at[kp])
            send(sm, a1.at[km], a1_sem.at[km], a=-1)
            if h > 1:
                send(sp, a1.at[kp], a1_sem.at[kp], a=1)
            else:
                q = t.parity(j)
                send(sp, a2.at[q], a2_sem.at[q], a=1)
    for j in (1, 0):
        s, k = own_b(0, j)
        take(s, a1.at[k], a1_sem.at[k])
        q = t.parity(j)
        take(s, a2.at[q], a2_sem.at[q])
        if j == 1:
            send(s, y1, y1_sem, j=1)
    take(sid(0, 0, 0), y1, y1_sem)
    sent = part.at[pl.ds(0, NSLOT - 1)]
    wait_for(sent, send_sem)


def column_of(row):
    n = row.shape[1]
    eye = lax.broadcasted_iota(jnp.int32, (n, n), 0) == lax.broadcasted_iota(jnp.int32, (n, n), 1)
    return jnp.sum(jnp.where(eye, jnp.broadcast_to(row, (n, n)), 0.0), axis=1, keepdims=True)


def kernel(
    x_ref, bias_ref, enc_hbm, ebias_ref, dec_hbm, other_ref, gate_ref,
    err_ref, mse_ref, gd_ref, ge_ref,
    enc, dec, xt, et, part, r1, r2, a1, a2, y1, act, pos2, cr, ys, yr, sq_z, sq_x, sq_y, sq_t,
    load_sem, ag_send, ag_recv, rs_send, r1_sem, r2_sem, a1_sem, a2_sem, y1_sem,
    ag2_send, ag2_recv, core_send, core_recv, yx_send, yx_recv, sq_send, sq_recv,
):
    x, y, z = place()
    dp = lax.axis_index("dp")
    core, half = lax.rem(dp, 2), lax.div(dp, 2)
    own = slot_id(x, y, z)
    width, rows = x_ref.shape
    lats = dec.shape[0]
    block = lats // gate_ref.shape[0]

    load_e = pltpu.make_async_copy(enc_hbm, enc, load_sem.at[0])
    load_d = pltpu.make_async_copy(dec_hbm, dec, load_sem.at[1])
    load_e.start()
    load_d.start()

    barrier = pltpu.get_barrier_semaphore()
    for k in range(1, NX):
        pl.semaphore_signal(barrier, inc=1, device_id={"lat": slot_id(x + k, y, z)}, device_id_type=MESH)
    for k in range(1, NZ):
        pl.semaphore_signal(barrier, inc=1, device_id={"lat": slot_id(x, y, z + k)}, device_id_type=MESH)
    for k in range(1, 8):
        pl.semaphore_signal(
            barrier,
            inc=1,
            device_id={"lat": slot_id(x, y + k // 4, z), "dp": lax.rem(dp + k, 4)},
            device_id_type=MESH,
        )
    bias_col = column_of(bias_ref[...].astype(F32))
    x_f = x_ref[...].astype(F32)
    xt[own] = (x_f - bias_col).astype(BF16)
    pl.semaphore_wait(barrier, NX - 1 + NZ - 1 + 7)

    for c in range(2):

        @pl.when(core == c)
        def _():
            gather_tree(xt, ag_send, ag_recv, c == 1)

    load_e.wait()
    load_d.wait()

    group = NSLOT // 8
    feats = group * width

    def pre_step(k, acc):
        w = enc[pl.ds(pl.multiple_of(k * feats, feats), feats), :]
        v = xt[pl.ds(k * group, group)].reshape(feats, rows)
        return acc + lax.dot_general(w, v, (((0,), (0,)), ((), ())), preferred_element_type=F32)

    pre = lax.fori_loop(0, 8, pre_step, jnp.zeros((lats, rows), F32))
    positive = jnp.maximum(pre + column_of(ebias_ref[...]), 0.0)
    gate = jnp.concatenate(
        [jnp.broadcast_to(gate_ref[i : i + 1, :].astype(F32), (block, rows)) for i in range(lats // block)], axis=0
    )
    gated = positive * gate
    act[...] = (positive * gated).astype(BF16)
    pos2[...] = 2.0 * gated

    def rec_step(k, carry):
        w = dec[:, pl.ds(pl.multiple_of(k * feats, feats), feats)]
        out = lax.dot_general(w, act[...], (((0,), (0,)), ((), ())), preferred_element_type=F32)
        part[pl.ds(k * group, group)] = out.reshape(group, width, rows)
        return carry

    lax.fori_loop(0, 8, rec_step, 0)

    for c in range(2):

        @pl.when(core == c)
        def _():
            scatter_tree(
                part, r1, r2, a1, a2, y1, rs_send, r1_sem, r2_sem, a1_sem, a2_sem, y1_sem, c == 1
            )

    error = part[own] + other_ref[...] + bias_col - x_f
    err_ref[...] = error
    et[own] = error.astype(BF16)
    sq = error * error
    tile = sum(sq[8 * i : 8 * i + 8] for i in range(width // 8))
    tile = sum(tile[:, 128 * i : 128 * i + 128] for i in range(rows // 128))
    total_rows = rows * 4
    tile = tile * (1.0 / (total_rows * width * NSLOT))

    def spread(dst, mine, level, value, peers):
        dst[mine] = value
        sq_t[level] = value
        for i, dev in enumerate(peers):
            pltpu.make_async_remote_copy(
                src_ref=sq_t.at[level],
                dst_ref=dst.at[mine],
                send_sem=sq_send.at[level],
                recv_sem=sq_recv.at[level],
                device_id=dev,
                device_id_type=MESH,
            ).start()

    def collect(dst, mine, level, n):
        view = dst.at[pl.ds(0, n - 1)]
        wait_for(view, sq_recv.at[level])
        wait_for(view, sq_send.at[level])
        return sum(dst[i] for i in range(n))

    spread(sq_z, z, 0, tile, [{"lat": slot_id(x, y, z + k)} for k in range(1, NZ)])

    for c in range(2):

        @pl.when(core == c)
        def _():
            gather_tree(et, ag2_send, ag2_recv, c == 1)

    tile = collect(sq_z, z, 0, NZ)
    spread(sq_x, x, 1, tile, [{"lat": slot_id(x + k, y, z)} for k in range(1, NX)])

    share = lats // 4
    other_core = lax.rem(core + 1, 2)

    def grad(lhs, rhs, base):
        def step(k, carry):
            v = rhs[pl.ds(k * group, group)].reshape(feats, rows)
            out = lax.dot_general(lhs, v, (((1,), (1,)), ((), ())), preferred_element_type=F32)
            for q in range(4):
                part[base + q * 8 + k] = out[q * share : (q + 1) * share, :]
            return carry

        lax.fori_loop(0, 8, step, 0)

    def core_copy(i, h):
        src = part.at[pl.ds(i * 32 + (h * 2 + other_core) * 8, 8)]
        return pltpu.make_async_remote_copy(
            src_ref=src,
            dst_ref=cr.at[i, h],
            send_sem=core_send.at[i, h],
            recv_sem=core_recv.at[i, h],
            device_id={"dp": half * 2 + other_core},
            device_id_type=MESH,
        )

    def y_copy(i):
        return pltpu.make_async_remote_copy(
            src_ref=ys.at[i],
            dst_ref=yr.at[i],
            send_sem=yx_send.at[i],
            recv_sem=yx_recv.at[i],
            device_id={"dp": (1 - half) * 2 + core},
            device_id_type=MESH,
        )

    def start_core(i):
        core_copy(i, 1 - half).start()
        core_copy(i, half).start()

    def start_y(i):
        h = 1 - half
        core_copy(i, h).wait_recv()
        base = i * 32 + (h * 2 + core) * 8

        def step(k, carry):
            ys[i, k] = (part[base + k] + cr[i, h, k]).astype(BF16)
            return carry

        lax.fori_loop(0, 8, step, 0)
        y_copy(i).start()

    def finish(i, out_ref):
        core_copy(i, half).wait_recv()
        y_copy(i).wait_recv()
        base = i * 32 + (half * 2 + core) * 8
        for k in range(8):
            out_ref[:, k * feats : (k + 1) * feats] = (part[base + k] + cr[i, half, k]) + yr[i, k].astype(F32)
        core_copy(i, 0).wait_send()
        core_copy(i, 1).wait_send()
        y_copy(i).wait_send()

    grad(act[...], et, 0)
    start_core(0)

    def dact_step(k, acc):
        w = dec[:, pl.ds(pl.multiple_of(k * feats, feats), feats)]
        v = et[pl.ds(k * group, group)].reshape(feats, rows)
        return acc + lax.dot_general(w, v, (((1,), (0,)), ((), ())), preferred_element_type=F32)

    dact = lax.fori_loop(0, 8, dact_step, jnp.zeros((lats, rows), F32))
    dpre = (dact * pos2[...]).astype(BF16)
    start_y(0)
    grad(dpre, xt, 32)
    start_core(1)
    tile = collect(sq_x, x, 1, NX)
    mine = y * 4 + dp
    spread(
        sq_y,
        mine,
        2,
        tile,
        [{"lat": slot_id(x, y + k // 4, z), "dp": lax.rem(dp + k, 4)} for k in range(1, 8)],
    )
    start_y(1)
    finish(0, gd_ref)
    tile = collect(sq_y, mine, 2, 8)
    mse_ref[...] = jnp.broadcast_to(jnp.sum(tile, keepdims=True), mse_ref.shape)
    finish(1, ge_ref)


def local(inputs, dec_bias, enc_weight, enc_bias, dec_weight, other_recon, active_blocks):
    rows, width = inputs.shape
    lats, features = dec_weight.shape
    share = lats // 4
    slots = (NSLOT, width, rows)
    vmem = pl.BlockSpec(memory_space=pltpu.VMEM)
    hbm = pl.BlockSpec(memory_space=pl.ANY)
    dma = pltpu.SemaphoreType.DMA
    error, mse, grad_dec, grad_enc = pl.pallas_call(
        kernel,
        name="sae_step",
        out_shape=(
            jax.ShapeDtypeStruct((width, rows), F32),
            jax.ShapeDtypeStruct((8, 128), F32),
            jax.ShapeDtypeStruct((share, features), F32),
            jax.ShapeDtypeStruct((share, features), F32),
        ),
        in_specs=[vmem, vmem, hbm, vmem, hbm, vmem, vmem],
        out_specs=(vmem, vmem, vmem, vmem),
        scratch_shapes=[
            pltpu.VMEM(enc_weight.shape, BF16),
            pltpu.VMEM(dec_weight.shape, BF16),
            pltpu.VMEM(slots, BF16),
            pltpu.VMEM(slots, BF16),
            pltpu.VMEM(slots, F32),
            pltpu.VMEM(slots, F32),
            pltpu.VMEM((2 * NZ, width, rows), F32),
            pltpu.VMEM((2 * NZ, width, rows), F32),
            pltpu.VMEM((2, width, rows), F32),
            pltpu.VMEM((width, rows), F32),
            pltpu.VMEM((lats, rows), BF16),
            pltpu.VMEM((lats, rows), F32),
            pltpu.VMEM((2, 2, 8, share, rows), F32),
            pltpu.VMEM((2, 8, share, rows), BF16),
            pltpu.VMEM((2, 8, share, rows), BF16),
            pltpu.VMEM((NZ, 8, 128), F32),
            pltpu.VMEM((NX, 8, 128), F32),
            pltpu.VMEM((8, 8, 128), F32),
            pltpu.VMEM((3, 8, 128), F32),
            dma((2,)),
            dma,
            dma((NSLOT,)),
            dma,
            dma((NSLOT,)),
            dma((2 * NZ,)),
            dma((2 * NZ,)),
            dma((2,)),
            dma,
            dma,
            dma((NSLOT,)),
            dma((2, 2)),
            dma((2, 2)),
            dma((2,)),
            dma((2,)),
            dma((3,)),
            dma((3,)),
        ],
        compiler_params=pltpu.CompilerParams(
            collective_id=0, has_side_effects=True, vmem_limit_bytes=60 * 2**20
        ),
    )(
        inputs.T,
        dec_bias.reshape(1, -1),
        enc_weight,
        enc_bias.reshape(1, -1),
        dec_weight,
        other_recon.T,
        active_blocks.T,
    )
    return error.T, mse[0, 0], grad_dec, grad_enc.T


def solution(mesh):
    placed = (
        P("dp", "lat"),
        P("lat"),
        P(None, "lat"),
        P("lat"),
        P("lat", None),
        P("dp", "lat"),
        P("dp", "lat"),
    )
    return jax.shard_map(
        local,
        mesh=mesh,
        in_specs=placed,
        out_specs=(P("dp", "lat"), P(), P(("lat", "dp"), None), P(None, ("lat", "dp"))),
        check_vma=False,
    )
```

```python
import functools

import jax
import jax.numpy as jnp
from jax import lax
from jax.experimental import pallas as pl
from jax.experimental.pallas import tpu as pltpu
from jax.sharding import PartitionSpec as P

MESH = pl.DeviceIdType.MESH
NX, NY, NZ = 4, 2, 8
NSLOT = NX * NY * NZ
BF16, F32 = jnp.bfloat16, jnp.float32


def place():
    lat = lax.axis_index("lat")
    return lax.div(lat, NY * NZ), lax.rem(lax.div(lat, NZ), NY), lax.rem(lat, NZ)


def slot_id(x, y, z):
    return (lax.rem(x + 2 * NX, NX) * NY + lax.rem(y + 2, NY)) * NZ + lax.rem(z + 2 * NZ, NZ)


def offset(k):
    half = lax.div(k + 1, 2)
    return jnp.where(lax.rem(k, 2) == 1, -half, half)


class Tree:
    def __init__(self, swap):
        self.swap = swap
        self.na, self.nb = (NZ, NX) if swap else (NX, NZ)
        self.x, self.y, self.z = place()

    def sid(self, a, b, j):
        if self.swap:
            return slot_id(self.x + b, self.y + j, self.z + a)
        return slot_id(self.x + a, self.y + j, self.z + b)

    def parity(self, j):
        return lax.rem(self.y + j, 2)

    def column(self, a, j):
        n = self.na
        me = self.z if self.swap else self.x
        return lax.rem(me + a + 2 * n, n) * 2 + self.parity(j)


def wait_for(ref, sem):
    pltpu.make_async_copy(ref, ref, sem).wait()


def gather_tree(buf, send_sem, recv_sem, swap):
    t = Tree(swap)
    na, nb, sid = t.na, t.nb, t.sid

    def send(s, a=0, b=0, j=0):
        pltpu.make_async_remote_copy(
            src_ref=buf.at[s],
            dst_ref=buf.at[s],
            send_sem=send_sem,
            recv_sem=recv_sem.at[s],
            device_id={"lat": sid(a, b, j)},
            device_id_type=MESH,
        ).start()

    def wait(s):
        wait_for(buf.at[s], recv_sem.at[s])

    own, other = sid(0, 0, 0), sid(0, 0, 1)
    send(own, j=1)
    for s in (own, other):
        if s is other:
            wait(other)
        send(s, a=1)
        send(s, a=-1)
        send(s, b=1)
        send(s, b=-1)
    for h in range(1, na // 2 + 1):
        for j in range(2):
            if h < na // 2:
                sm, sp = sid(-h, 0, j), sid(h, 0, j)
                wait(sm)
                if h + 1 < na // 2:
                    send(sm, a=1)
                send(sm, b=1)
                send(sm, b=-1)
                wait(sp)
                if h + 1 < na // 2:
                    send(sp, a=-1)
                send(sp, b=1)
                send(sp, b=-1)
                if h + 1 == na // 2:
                    pl.when(t.parity(j) == 0)(functools.partial(send, sm, a=1))
                    pl.when(t.parity(j) == 1)(functools.partial(send, sp, a=-1))
            else:
                s = sid(h, 0, j)
                wait(s)
                send(s, b=1)
                send(s, b=-1)

    def hop(h, c, carry):
        a, j = offset(lax.div(c, 2)), lax.rem(c, 2)
        if h == nb // 2:
            wait(sid(a, h, j))
            return carry
        sm, sp = sid(a, -h, j), sid(a, h, j)
        wait(sm)
        if h + 1 < nb // 2:
            send(sm, b=1)
        else:
            pl.when(t.parity(j) == 0)(functools.partial(send, sm, b=1))
        wait(sp)
        if h + 1 < nb // 2:
            send(sp, b=-1)
        else:
            pl.when(t.parity(j) == 1)(functools.partial(send, sp, b=-1))
        return carry

    for h in range(1, nb // 2 + 1):
        lax.fori_loop(0, 2 * na, functools.partial(hop, h), 0)
    sent = buf.at[pl.ds(0, NSLOT - 1)]
    wait_for(sent, send_sem)


def over_tiles(v):
    w, r = v.shape
    return [[v[8 * i : 8 * i + 8, 128 * k : 128 * k + 128] for k in range(r // 128)] for i in range(w // 8)]


def tiled(tile, shape):
    row = jnp.concatenate([tile] * (shape[1] // 128), axis=1)
    return jnp.concatenate([row] * (shape[0] // 8), axis=0)


LEVELS = 32000.0


def encode(v):
    top = functools.reduce(
        jnp.maximum, [functools.reduce(jnp.maximum, [jnp.abs(t) for t in line]) for line in over_tiles(v)]
    )
    top = jnp.maximum(top, 1e-30)
    return jnp.round(v * tiled(LEVELS / top, v.shape)).astype(jnp.int16), top * (1.0 / LEVELS)


def decode(q, scale):
    return q.astype(F32) * tiled(scale, q.shape)


def scatter_tree(part, out, r1, r2, a1, a2, y1, send_sem, r1_sem, r2_sem, a1_sem, a2_sem, y1_sem, swap):
    t = Tree(swap)
    na, nb, sid = t.na, t.nb, t.sid

    def send(s, dst, k, sem, a=0, b=0, j=0):
        out[0][s], out[1][s] = encode(part[s])
        for i in range(2):
            pltpu.make_async_remote_copy(
                src_ref=out[i].at[s],
                dst_ref=dst[i].at[k],
                send_sem=send_sem.at[i],
                recv_sem=sem.at[i, k],
                device_id={"lat": sid(a, b, j)},
                device_id_type=MESH,
            ).start()

    def take(s, ref, k, sem):
        for i in range(2):
            wait_for(ref[i].at[k], sem.at[i, k])
        part[s] += decode(ref[0][k], ref[1][k])

    def col(c):
        k = na - 1 - lax.div(c, 2)
        return offset(k), lax.rem(c, 2)

    far = nb // 2

    def first(c, carry):
        a, j = col(c)
        s = sid(a, far, j)
        pl.when(t.parity(j) == 0)(functools.partial(send, s, r1, s, r1_sem, b=-1))
        pl.when(t.parity(j) == 1)(functools.partial(send, s, r1, s, r1_sem, b=1))
        return carry

    def hop(h, c, carry):
        a, j = col(c)
        sm, sp = sid(a, -h, j), sid(a, h, j)
        if h == far - 1:
            pl.when(t.parity(j) == 0)(functools.partial(take, sm, r1, sm, r1_sem))
            pl.when(t.parity(j) == 1)(functools.partial(take, sp, r1, sp, r1_sem))
        else:
            take(sm, r1, sm, r1_sem)
        send(sm, r1, sm, r1_sem, b=-1)
        if h < far - 1:
            take(sp, r1, sp, r1_sem)
        if h > 1:
            send(sp, r1, sp, r1_sem, b=1)
        else:
            send(sp, r2, t.column(a, j), r2_sem, b=1)
        return carry

    lax.fori_loop(0, 2 * na, first, 0)
    for h in range(far - 1, 0, -1):
        lax.fori_loop(0, 2 * na, functools.partial(hop, h), 0)

    def own_b(a, j):
        s, k = sid(a, 0, j), t.column(a, j)
        take(s, r1, s, r1_sem)
        take(s, r2, k, r2_sem)
        return s, k

    fara = na // 2
    for j in range(2):
        s, k = own_b(fara, j)
        pl.when(t.parity(j) == 0)(functools.partial(send, s, a1, k, a1_sem, a=-1))
        pl.when(t.parity(j) == 1)(functools.partial(send, s, a1, k, a1_sem, a=1))
    for h in range(fara - 1, 0, -1):
        for j in range(2):
            sm, km = own_b(-h, j)
            sp, kp = own_b(h, j)
            if h == fara - 1:
                pl.when(t.parity(j) == 0)(functools.partial(take, sm, a1, km, a1_sem))
                pl.when(t.parity(j) == 1)(functools.partial(take, sp, a1, kp, a1_sem))
            else:
                take(sm, a1, km, a1_sem)
                take(sp, a1, kp, a1_sem)
            send(sm, a1, km, a1_sem, a=-1)
            if h > 1:
                send(sp, a1, kp, a1_sem, a=1)
            else:
                send(sp, a2, t.parity(j), a2_sem, a=1)
    for j in (1, 0):
        s, k = own_b(0, j)
        take(s, a1, k, a1_sem)
        take(s, a2, t.parity(j), a2_sem)
        if j == 1:
            send(s, y1, 0, y1_sem, j=1)
    take(sid(0, 0, 0), y1, 0, y1_sem)
    for i in range(2):
        wait_for(out[i].at[pl.ds(0, NSLOT - 1)], send_sem.at[i])


def column_of(row):
    n = row.shape[1]
    eye = lax.broadcasted_iota(jnp.int32, (n, n), 0) == lax.broadcasted_iota(jnp.int32, (n, n), 1)
    return jnp.sum(jnp.where(eye, jnp.broadcast_to(row, (n, n)), 0.0), axis=1, keepdims=True)


def kernel(
    x_ref, bias_ref, enc_hbm, ebias_ref, dec_hbm, other_ref, gate_ref,
    err_ref, mse_ref, gd_ref, ge_ref,
    enc, dec, xt, et, part, out_q, out_s, r1_q, r1_s, r2_q, r2_s, a1_q, a1_s, a2_q, a2_s, y1_q, y1_s, act, pos2, cr, ys, yr, sq_z, sq_x, sq_y, sq_t,
    load_sem, ag_send, ag_recv, rs_send, r1_sem, r2_sem, a1_sem, a2_sem, y1_sem,
    ag2_send, ag2_recv, core_send, core_recv, yx_send, yx_recv, sq_send, sq_recv,
):
    x, y, z = place()
    dp = lax.axis_index("dp")
    core, half = lax.rem(dp, 2), lax.div(dp, 2)
    own = slot_id(x, y, z)
    width, rows = x_ref.shape
    lats = dec.shape[0]
    block = lats // gate_ref.shape[0]

    load_e = pltpu.make_async_copy(enc_hbm, enc, load_sem.at[0])
    load_d = pltpu.make_async_copy(dec_hbm, dec, load_sem.at[1])
    load_e.start()
    load_d.start()

    barrier = pltpu.get_barrier_semaphore()
    for k in range(1, NX):
        pl.semaphore_signal(barrier, inc=1, device_id={"lat": slot_id(x + k, y, z)}, device_id_type=MESH)
    for k in range(1, NZ):
        pl.semaphore_signal(barrier, inc=1, device_id={"lat": slot_id(x, y, z + k)}, device_id_type=MESH)
    for k in range(1, 8):
        pl.semaphore_signal(
            barrier,
            inc=1,
            device_id={"lat": slot_id(x, y + k // 4, z), "dp": lax.rem(dp + k, 4)},
            device_id_type=MESH,
        )
    bias_col = column_of(bias_ref[...].astype(F32))
    x_f = x_ref[...].astype(F32)
    xt[own] = (x_f - bias_col).astype(BF16)
    pl.semaphore_wait(barrier, NX - 1 + NZ - 1 + 7)

    for c in range(2):

        @pl.when(core == c)
        def _():
            gather_tree(xt, ag_send, ag_recv, c == 1)

    load_e.wait()
    load_d.wait()

    group = NSLOT // 8
    feats = group * width

    def pre_step(k, acc):
        w = enc[pl.ds(pl.multiple_of(k * feats, feats), feats), :]
        v = xt[pl.ds(k * group, group)].reshape(feats, rows)
        return acc + lax.dot_general(w, v, (((0,), (0,)), ((), ())), preferred_element_type=F32)

    pre = lax.fori_loop(0, 8, pre_step, jnp.zeros((lats, rows), F32))
    positive = jnp.maximum(pre + column_of(ebias_ref[...]), 0.0)
    gate = jnp.concatenate(
        [jnp.broadcast_to(gate_ref[i : i + 1, :].astype(F32), (block, rows)) for i in range(lats // block)], axis=0
    )
    gated = positive * gate
    act[...] = (positive * gated).astype(BF16)
    pos2[...] = 2.0 * gated

    def rec_step(k, carry):
        w = dec[:, pl.ds(pl.multiple_of(k * feats, feats), feats)]
        out = lax.dot_general(w, act[...], (((0,), (0,)), ((), ())), preferred_element_type=F32)
        part[pl.ds(k * group, group)] = out.reshape(group, width, rows)
        return carry

    lax.fori_loop(0, 8, rec_step, 0)

    for c in range(2):

        @pl.when(core == c)
        def _():
            scatter_tree(
                part, (out_q, out_s), (r1_q, r1_s), (r2_q, r2_s), (a1_q, a1_s), (a2_q, a2_s), (y1_q, y1_s),
                rs_send, r1_sem, r2_sem, a1_sem, a2_sem, y1_sem, c == 1,
            )

    error = part[own] + other_ref[...] + bias_col - x_f
    err_ref[...] = error
    et[own] = error.astype(BF16)
    sq = error * error
    tile = sum(sq[8 * i : 8 * i + 8] for i in range(width // 8))
    tile = sum(tile[:, 128 * i : 128 * i + 128] for i in range(rows // 128))
    total_rows = rows * 4
    tile = tile * (1.0 / (total_rows * width * NSLOT))

    def spread(dst, mine, level, value, peers):
        dst[mine] = value
        sq_t[level] = value
        for i, dev in enumerate(peers):
            pltpu.make_async_remote_copy(
                src_ref=sq_t.at[level],
                dst_ref=dst.at[mine],
                send_sem=sq_send.at[level],
                recv_sem=sq_recv.at[level],
                device_id=dev,
                device_id_type=MESH,
            ).start()

    def collect(dst, mine, level, n):
        view = dst.at[pl.ds(0, n - 1)]
        wait_for(view, sq_recv.at[level])
        wait_for(view, sq_send.at[level])
        return sum(dst[i] for i in range(n))

    spread(sq_z, z, 0, tile, [{"lat": slot_id(x, y, z + k)} for k in range(1, NZ)])

    for c in range(2):

        @pl.when(core == c)
        def _():
            gather_tree(et, ag2_send, ag2_recv, c == 1)

    tile = collect(sq_z, z, 0, NZ)
    spread(sq_x, x, 1, tile, [{"lat": slot_id(x + k, y, z)} for k in range(1, NX)])

    share = lats // 4
    other_core = lax.rem(core + 1, 2)

    def grad(lhs, rhs, base):
        def step(k, carry):
            v = rhs[pl.ds(k * group, group)].reshape(feats, rows)
            out = lax.dot_general(lhs, v, (((1,), (1,)), ((), ())), preferred_element_type=F32)
            for q in range(4):
                part[base + q * 8 + k] = out[q * share : (q + 1) * share, :]
            return carry

        lax.fori_loop(0, 8, step, 0)

    def core_copy(i, h):
        src = part.at[pl.ds(i * 32 + (h * 2 + other_core) * 8, 8)]
        return pltpu.make_async_remote_copy(
            src_ref=src,
            dst_ref=cr.at[i, h],
            send_sem=core_send.at[i, h],
            recv_sem=core_recv.at[i, h],
            device_id={"dp": half * 2 + other_core},
            device_id_type=MESH,
        )

    def y_copy(i):
        return pltpu.make_async_remote_copy(
            src_ref=ys.at[i],
            dst_ref=yr.at[i],
            send_sem=yx_send.at[i],
            recv_sem=yx_recv.at[i],
            device_id={"dp": (1 - half) * 2 + core},
            device_id_type=MESH,
        )

    def start_core(i):
        core_copy(i, 1 - half).start()
        core_copy(i, half).start()

    def start_y(i):
        h = 1 - half
        core_copy(i, h).wait_recv()
        base = i * 32 + (h * 2 + core) * 8

        def step(k, carry):
            ys[i, k] = (part[base + k] + cr[i, h, k]).astype(BF16)
            return carry

        lax.fori_loop(0, 8, step, 0)
        y_copy(i).start()

    def finish(i, out_ref):
        core_copy(i, half).wait_recv()
        y_copy(i).wait_recv()
        base = i * 32 + (half * 2 + core) * 8
        for k in range(8):
            out_ref[:, k * feats : (k + 1) * feats] = (part[base + k] + cr[i, half, k]) + yr[i, k].astype(F32)
        core_copy(i, 0).wait_send()
        core_copy(i, 1).wait_send()
        y_copy(i).wait_send()

    grad(act[...], et, 0)
    start_core(0)

    def dact_step(k, acc):
        w = dec[:, pl.ds(pl.multiple_of(k * feats, feats), feats)]
        v = et[pl.ds(k * group, group)].reshape(feats, rows)
        return acc + lax.dot_general(w, v, (((1,), (0,)), ((), ())), preferred_element_type=F32)

    dact = lax.fori_loop(0, 8, dact_step, jnp.zeros((lats, rows), F32))
    dpre = (dact * pos2[...]).astype(BF16)
    start_y(0)
    grad(dpre, xt, 32)
    start_core(1)
    tile = collect(sq_x, x, 1, NX)
    mine = y * 4 + dp
    spread(
        sq_y,
        mine,
        2,
        tile,
        [{"lat": slot_id(x, y + k // 4, z), "dp": lax.rem(dp + k, 4)} for k in range(1, 8)],
    )
    start_y(1)
    finish(0, gd_ref)
    tile = collect(sq_y, mine, 2, 8)
    mse_ref[...] = jnp.broadcast_to(jnp.sum(tile, keepdims=True), mse_ref.shape)
    finish(1, ge_ref)


def local(inputs, dec_bias, enc_weight, enc_bias, dec_weight, other_recon, active_blocks):
    rows, width = inputs.shape
    lats, features = dec_weight.shape
    share = lats // 4
    slots = (NSLOT, width, rows)
    vmem = pl.BlockSpec(memory_space=pltpu.VMEM)
    hbm = pl.BlockSpec(memory_space=pl.ANY)
    dma = pltpu.SemaphoreType.DMA

    def coded(n):
        return pltpu.VMEM((n, width, rows), jnp.int16), pltpu.VMEM((n, 8, 128), F32)

    error, mse, grad_dec, grad_enc = pl.pallas_call(
        kernel,
        name="sae_step",
        out_shape=(
            jax.ShapeDtypeStruct((width, rows), F32),
            jax.ShapeDtypeStruct((8, 128), F32),
            jax.ShapeDtypeStruct((share, features), F32),
            jax.ShapeDtypeStruct((share, features), F32),
        ),
        in_specs=[vmem, vmem, hbm, vmem, hbm, vmem, vmem],
        out_specs=(vmem, vmem, vmem, vmem),
        scratch_shapes=[
            pltpu.VMEM(enc_weight.shape, BF16),
            pltpu.VMEM(dec_weight.shape, BF16),
            pltpu.VMEM(slots, BF16),
            pltpu.VMEM(slots, BF16),
            pltpu.VMEM(slots, F32),
            *coded(NSLOT),
            *coded(NSLOT),
            *coded(2 * NZ),
            *coded(2 * NZ),
            *coded(2),
            *coded(1),
            pltpu.VMEM((lats, rows), BF16),
            pltpu.VMEM((lats, rows), F32),
            pltpu.VMEM((2, 2, 8, share, rows), F32),
            pltpu.VMEM((2, 8, share, rows), BF16),
            pltpu.VMEM((2, 8, share, rows), BF16),
            pltpu.VMEM((NZ, 8, 128), F32),
            pltpu.VMEM((NX, 8, 128), F32),
            pltpu.VMEM((8, 8, 128), F32),
            pltpu.VMEM((3, 8, 128), F32),
            dma((2,)),
            dma,
            dma((NSLOT,)),
            dma((2,)),
            dma((2, NSLOT)),
            dma((2, 2 * NZ)),
            dma((2, 2 * NZ)),
            dma((2, 2)),
            dma((2, 1)),
            dma,
            dma((NSLOT,)),
            dma((2, 2)),
            dma((2, 2)),
            dma((2,)),
            dma((2,)),
            dma((3,)),
            dma((3,)),
        ],
        compiler_params=pltpu.CompilerParams(
            collective_id=0, has_side_effects=True, vmem_limit_bytes=60 * 2**20
        ),
    )(
        inputs.T,
        dec_bias.reshape(1, -1),
        enc_weight,
        enc_bias.reshape(1, -1),
        dec_weight,
        other_recon.T,
        active_blocks.T,
    )
    return error.T, mse[0, 0], grad_dec, grad_enc.T


def solution(mesh):
    placed = (
        P("dp", "lat"),
        P("lat"),
        P(None, "lat"),
        P("lat"),
        P("lat", None),
        P("dp", "lat"),
        P("dp", "lat"),
    )
    return jax.shard_map(
        local,
        mesh=mesh,
        in_specs=placed,
        out_specs=(P("dp", "lat"), P(), P(("lat", "dp"), None), P(None, ("lat", "dp"))),
        check_vma=False,
    )
```

```python
import functools

import jax
import jax.numpy as jnp
from jax import lax
from jax.experimental import pallas as pl
from jax.experimental.pallas import tpu as pltpu
from jax.sharding import PartitionSpec as P

MESH = pl.DeviceIdType.MESH
NX, NY, NZ = 4, 2, 8
NSLOT = NX * NY * NZ
GROUP = 8
BF16, F32 = jnp.bfloat16, jnp.float32


def place():
    lat = lax.axis_index("lat")
    return lax.div(lat, NY * NZ), lax.rem(lax.div(lat, NZ), NY), lax.rem(lat, NZ)


def slot_id(x, y, z):
    return (lax.rem(x + 2 * NX, NX) * NY + lax.rem(y + 2, NY)) * NZ + lax.rem(z + 2 * NZ, NZ)


def offset(k):
    half = lax.div(k + 1, 2)
    return jnp.where(lax.rem(k, 2) == 1, -half, half)


class Tree:
    def __init__(self, t):
        self.t = t
        self.na, self.nb = (NZ, NX) if t else (NX, NZ)
        self.x, self.y, self.z = place()

    def sid(self, a, b, j):
        if self.t:
            return slot_id(self.x + b, self.y + j, self.z + a)
        return slot_id(self.x + a, self.y + j, self.z + b)

    def parity(self, j):
        return lax.rem(self.y + j, 2)

    def row(self, a):
        n = self.na
        return lax.rem((self.z if self.t else self.x) + a + 2 * n, n)

    def column(self, a, j):
        return self.row(a) * 2 + self.parity(j)

    def chunks(self, b):
        if self.t:
            base = lax.rem(self.x + b + 2 * NX, NX) * NY
            return [(base + i, [(base + i) * GROUP + k for k in range(GROUP)]) for i in range(NY)]
        base = lax.rem(self.z + b + 2 * NZ, NZ)
        return [(base, [base + NZ * k for k in range(GROUP)])]


def wait_for(ref, sem):
    pltpu.make_async_copy(ref, ref, sem).wait()


def each(n, *bodies):
    def step(c, carry):
        for body in bodies:
            body(c)
        return carry

    lax.fori_loop(0, n, step, 0)


class Gather:
    def __init__(self, t, buf, send_sem, recv_sem):
        self.tree = Tree(t)
        self.buf, self.send_sem, self.recv_sem = buf.at[t], send_sem.at[t], recv_sem.at[t]

    def send(self, s, a=0, b=0, j=0):
        pltpu.make_async_remote_copy(
            src_ref=self.buf.at[s],
            dst_ref=self.buf.at[s],
            send_sem=self.send_sem,
            recv_sem=self.recv_sem.at[s],
            device_id={"lat": self.tree.sid(a, b, j)},
            device_id_type=MESH,
        ).start()

    def wait(self, s):
        wait_for(self.buf.at[s], self.recv_sem.at[s])

    def onward(self, s):
        self.send(s, b=1)
        self.send(s, b=-1)

    def own(self):
        s = self.tree.sid(0, 0, 0)
        self.send(s, a=1)
        self.send(s, a=-1)
        self.send(s, j=1)
        self.onward(s)

    def from_y(self, a):
        s = self.tree.sid(a, 0, 1)
        self.wait(s)
        self.onward(s)

    def ring_a(self, h):
        t = self.tree
        far = t.na // 2
        for d in (-1, 1) if h < far else (1,):
            s = t.sid(d * h, 0, 0)
            self.wait(s)
            if h + 1 < far:
                self.send(s, a=-d)
            elif h < far:
                pl.when(t.y == (d + 1) // 2)(functools.partial(self.send, s, a=-d))
            self.send(s, j=1)
            self.onward(s)
        self.from_y(1 - h)
        if h > 1:
            self.from_y(h - 1)
        if h == far:
            self.from_y(h)

    def ring_b(self, h, c):
        t = self.tree
        far = t.nb // 2
        a, j = offset(lax.div(c, 2)), lax.rem(c, 2)
        if h == far:
            self.wait(t.sid(a, h, j))
            return
        for d in (-1, 1):
            s = t.sid(a, d * h, j)
            self.wait(s)
            if h + 1 < far:
                self.send(s, b=-d)
            else:
                pl.when(t.parity(j) == (d + 1) // 2)(functools.partial(self.send, s, b=-d))

    def end(self):
        wait_for(self.buf.at[pl.ds(0, NSLOT - 1)], self.send_sem)


def gather(buf, send_sem, recv_sem, eat, idle):
    p, q = (Gather(t, buf, send_sem, recv_sem) for t in range(2))

    def eat_all(g, *offsets):
        for b in offsets:
            for index, slots in g.tree.chunks(b):
                eat(g.tree.t, index, slots)

    p.own()
    q.own()
    p.ring_a(1)
    q.ring_a(1)
    p.ring_a(2)
    q.ring_a(2)
    q.ring_a(3)
    each(8, lambda c: p.ring_b(1, c))
    q.ring_a(4)
    idle(0)
    eat_all(p, 0)
    each(8, lambda c: p.ring_b(2, c), lambda c: q.ring_b(1, c))
    eat_all(p, -1, 1)
    eat_all(q, 0)
    idle(1)
    each(8, lambda c: p.ring_b(3, c), lambda c: q.ring_b(1, c + 8))
    eat_all(p, -2, 2)
    eat_all(q, -1, 1)
    idle(2)
    each(8, lambda c: p.ring_b(4, c), lambda c: q.ring_b(2, c))
    each(8, lambda c: q.ring_b(2, c + 8))
    eat_all(p, -3, 3, 4)
    eat_all(q, 2)
    idle(3)
    p.end()
    q.end()


def tiled(row, shape):
    return jnp.broadcast_to(jnp.concatenate([row] * (shape[1] // 128), axis=1), shape)


LEVELS = 32000.0


def encode(v):
    size = jnp.abs(v)
    top = functools.reduce(jnp.maximum, [size[:, i : i + 128] for i in range(0, v.shape[1], 128)])
    top = jnp.maximum(jnp.max(top, axis=0, keepdims=True), 1e-30)
    return jnp.round(v * tiled(LEVELS / top, v.shape)).astype(jnp.int16), top * (1.0 / LEVELS)


def decode(q, scale):
    return q.astype(F32) * tiled(scale, q.shape)


class Scatter:
    def __init__(self, t, part, out, r1, r2, y1, a1, a2, send_sem, r1_sem, r2_sem, y1_sem, a1_sem, a2_sem):
        self.tree = Tree(t)
        self.part = part.at[t]
        self.out, self.send_sem = [o.at[t] for o in out], [send_sem.at[t, i] for i in range(2)]
        bufs = {"r1": (r1, r1_sem), "r2": (r2, r2_sem), "y1": (y1, y1_sem), "a1": (a1, a1_sem), "a2": (a2, a2_sem)}
        self.bufs = {
            name: ([r.at[t] for r in refs], [sem.at[t, i] for i in range(2)]) for name, (refs, sem) in bufs.items()
        }

    def send(self, s, name, k, a=0, b=0, j=0):
        self.out[0][s], self.out[1][s] = encode(self.part[s])
        refs, sems = self.bufs[name]
        for i in range(2):
            pltpu.make_async_remote_copy(
                src_ref=self.out[i].at[s],
                dst_ref=refs[i].at[k],
                send_sem=self.send_sem[i],
                recv_sem=sems[i].at[k],
                device_id={"lat": self.tree.sid(a, b, j)},
                device_id_type=MESH,
            ).start()

    def take(self, s, name, k):
        refs, sems = self.bufs[name]
        for i in range(2):
            wait_for(refs[i].at[k], sems[i].at[k])
        self.part[s] += decode(refs[0][k], refs[1][k])

    def col(self, c):
        return offset(self.tree.na - 1 - lax.div(c, 2)), 1 - lax.rem(c, 2)

    def first(self, c):
        t = self.tree
        a, j = self.col(c)
        s = t.sid(a, t.nb // 2, j)
        for d in (-1, 1):
            pl.when(t.parity(j) == (d + 1) // 2)(functools.partial(self.send, s, "r1", s, b=d))

    def hop(self, h, c):
        t = self.tree
        a, j = self.col(c)
        for d in (-1, 1):
            s = t.sid(a, d * h, j)
            if h == t.nb // 2 - 1:
                pl.when(t.parity(j) == (d + 1) // 2)(functools.partial(self.take, s, "r1", s))
            else:
                self.take(s, "r1", s)
            if h == 1 and d == 1:
                self.send(s, "r2", t.column(a, j), b=d)
            else:
                self.send(s, "r1", s, b=d)

    def own_b(self, a, j):
        s = self.tree.sid(a, 0, j)
        self.take(s, "r1", s)
        self.take(s, "r2", self.tree.column(a, j))
        return s

    def to_y(self, *offsets):
        for a in offsets:
            self.send(self.own_b(a, 1), "y1", self.tree.row(a), j=1)

    def with_y(self, a):
        s, k = self.own_b(a, 0), self.tree.row(a)
        self.take(s, "y1", k)
        return s, k

    def ring_a(self, h):
        t = self.tree
        far = t.na // 2
        if h == far:
            s, k = self.with_y(h)
            for d in (-1, 1):
                pl.when(t.y == (d + 1) // 2)(functools.partial(self.send, s, "a1", k, a=d))
            return
        if h == 0:
            s, k = self.with_y(0)
            self.take(s, "a1", k)
            self.take(s, "a2", 0)
            return
        for d in (-1, 1):
            s, k = self.with_y(d * h)
            if h == far - 1:
                pl.when(t.y == (d + 1) // 2)(functools.partial(self.take, s, "a1", k))
            else:
                self.take(s, "a1", k)
            if h == 1 and d == 1:
                self.send(s, "a2", 0, a=d)
            else:
                self.send(s, "a1", k, a=d)

    def end(self):
        for i in range(2):
            wait_for(self.out[i].at[pl.ds(0, NSLOT - 1)], self.send_sem[i])


def scatter(make, *refs):
    p, q = (Scatter(t, *refs) for t in range(2))

    def make_all(g, *offsets):
        for b in offsets:
            for _, slots in g.tree.chunks(b):
                make(g.tree.t, slots)

    make_all(p, 4)
    make_all(q, 2)
    each(8, p.first, q.first)
    make_all(p, -3, 3)
    each(8, lambda c: p.hop(3, c), lambda c: q.first(c + 8))
    make_all(q, -1, 1)
    make_all(p, -2, 2)
    each(8, lambda c: p.hop(2, c), lambda c: q.hop(1, c))
    make_all(p, -1, 1, 0)
    make_all(q, 0)
    each(8, lambda c: p.hop(1, c), lambda c: q.hop(1, c + 8))
    q.to_y(4, -3, 3)
    p.to_y(2, -1, 1)
    q.ring_a(4)
    q.to_y(-2, 2)
    p.ring_a(2)
    q.ring_a(3)
    q.to_y(-1, 1)
    p.to_y(0)
    q.ring_a(2)
    p.ring_a(1)
    q.to_y(0)
    q.ring_a(1)
    p.ring_a(0)
    q.ring_a(0)
    p.end()
    q.end()


def column_of(row):
    n = row.shape[1]
    eye = lax.broadcasted_iota(jnp.int32, (n, n), 0) == lax.broadcasted_iota(jnp.int32, (n, n), 1)
    return jnp.sum(jnp.where(eye, jnp.broadcast_to(row, (n, n)), 0.0), axis=1, keepdims=True)


def kernel(
    x_ref, bias_ref, enc_hbm, ebias_ref, dec_hbm, other_ref, gate_ref,
    err_ref, mse_ref, own_out, far_out,
    enc, dec, dec_t, xt, et, part, out_q, out_s, r1_q, r1_s, r2_q, r2_s, y1_q, y1_s, a1_q, a1_s, a2_q, a2_s,
    pre, act, pos2, dact, grads, cr, ys, kept, sq_z, sq_x, sq_y, sq_t,
    load_sem, ag_send, ag_recv, rs_send, r1_sem, r2_sem, y1_sem, a1_sem, a2_sem,
    ag2_send, ag2_recv, core_send, core_recv, yx_send, yx_recv, keep_sem, sq_send, sq_recv,
):
    x, y, z = place()
    dp = lax.axis_index("dp")
    core, half = lax.rem(dp, 2), lax.div(dp, 2)
    own = slot_id(x, y, z)
    width, rows = x_ref.shape
    tall = width // 2
    lats = dec.shape[0]
    block = lats // gate_ref.shape[0]

    loads = [pltpu.make_async_copy(enc_hbm.at[:, t], enc.at[t], load_sem.at[t]) for t in range(2)]
    loads.append(pltpu.make_async_copy(dec_hbm, dec, load_sem.at[2]))
    for load in loads:
        load.start()

    barrier = pltpu.get_barrier_semaphore()
    for k in range(1, NX):
        pl.semaphore_signal(barrier, inc=1, device_id={"lat": slot_id(x + k, y, z)}, device_id_type=MESH)
    for k in range(1, NZ):
        pl.semaphore_signal(barrier, inc=1, device_id={"lat": slot_id(x, y, z + k)}, device_id_type=MESH)
    for k in range(1, 8):
        pl.semaphore_signal(
            barrier,
            inc=1,
            device_id={"lat": slot_id(x, y + k // 4, z), "dp": lax.rem(dp + k, 4)},
            device_id_type=MESH,
        )
    bias_col = column_of(bias_ref[...].astype(F32))
    x_f = x_ref[...].astype(F32)
    centered = (x_f - bias_col).astype(BF16)
    for t in range(2):
        xt[t, own] = centered[t * tall : (t + 1) * tall]
    pl.semaphore_wait(barrier, NX - 1 + NZ - 1 + 7)

    def stack(ref, t, slots):
        return jnp.concatenate([ref[t, s] for s in slots], axis=0)

    def encode_chunk(t, index, slots):
        pre[...] += lax.dot_general(
            stack(enc, t, slots), stack(xt, t, slots), (((0,), (0,)), ((), ())), preferred_element_type=F32
        )

    def turn(k):
        if k == 0:
            for load in loads:
                load.wait()
            pre[...] = jnp.broadcast_to(column_of(ebias_ref[...]), pre.shape)
        if k == 1:
            for i in range(NSLOT // 2):
                both = dec[:, 2 * i * width : 2 * (i + 1) * width].T
                for n in range(4):
                    dec_t[n % 2, 2 * i + n // 2] = both[n * tall : (n + 1) * tall]

    gather(xt, ag_send, ag_recv, encode_chunk, turn)

    positive = jnp.maximum(pre[...], 0.0)
    gate = jnp.concatenate(
        [jnp.broadcast_to(gate_ref[i : i + 1, :].astype(F32), (block, rows)) for i in range(lats // block)], axis=0
    )
    gated = positive * gate
    act[...] = (positive * gated).astype(BF16)
    pos2[...] = 2.0 * gated

    def decode_chunk(t, slots):
        out = jnp.dot(stack(dec_t, t, slots), act[...], preferred_element_type=F32)
        for i, s in enumerate(slots):
            part[t, s] = out[i * tall : (i + 1) * tall]

    scatter(
        decode_chunk, part, (out_q, out_s), (r1_q, r1_s), (r2_q, r2_s), (y1_q, y1_s), (a1_q, a1_s), (a2_q, a2_s),
        rs_send, r1_sem, r2_sem, y1_sem, a1_sem, a2_sem,
    )

    total = jnp.concatenate([part[t, own] for t in range(2)], axis=0)
    error = total + other_ref[...] + bias_col - x_f
    err_ref[...] = error
    for t in range(2):
        et[t, own] = error[t * tall : (t + 1) * tall].astype(BF16)
    sq = error * error
    tile = sum(sq[8 * i : 8 * i + 8] for i in range(width // 8))
    tile = sum(tile[:, 128 * i : 128 * i + 128] for i in range(rows // 128))
    tile = tile * (1.0 / (rows * 4 * width * NSLOT))

    def spread(dst, mine, level, value, peers):
        dst[mine] = value
        sq_t[level] = value
        for dev in peers:
            pltpu.make_async_remote_copy(
                src_ref=sq_t.at[level],
                dst_ref=dst.at[mine],
                send_sem=sq_send.at[level],
                recv_sem=sq_recv.at[level],
                device_id=dev,
                device_id_type=MESH,
            ).start()

    def collect(dst, level, n):
        view = dst.at[pl.ds(0, n - 1)]
        wait_for(view, sq_recv.at[level])
        wait_for(view, sq_send.at[level])
        return sum(dst[i] for i in range(n))

    share = lats // 4
    other_core = lax.rem(core + 1, 2)

    def core_copy(i, t, index):
        return pltpu.make_async_remote_copy(
            src_ref=grads.at[i, t, index, other_core],
            dst_ref=cr.at[i, t, index],
            send_sem=core_send.at[i, t, index],
            recv_sem=core_recv.at[i, t, index],
            device_id={"dp": half * 2 + other_core},
            device_id_type=MESH,
        )

    def y_copy(i, t, index):
        return pltpu.make_async_remote_copy(
            src_ref=ys.at[i, t, index],
            dst_ref=far_out.at[i, t, index],
            send_sem=yx_send.at[i, t, index],
            recv_sem=yx_recv.at[i, t, index],
            device_id={"dp": (1 - half) * 2 + core},
            device_id_type=MESH,
        )

    def partial(i, t, index, slots, lhs, ref):
        out = lax.dot_general(lhs, stack(ref, t, slots), (((1,), (1,)), ((), ())), preferred_element_type=F32)
        for h in range(2):
            for c in range(2):
                n = h * 2 + c
                grads[i, t, index, c, h] = out[n * share : (n + 1) * share]
        core_copy(i, t, index).start()

    def exchange(i, t, index):
        core_copy(i, t, index).wait_recv()
        ys[i, t, index] = (grads[i, t, index, core, 1 - half] + cr[i, t, index, 1 - half]).astype(BF16)
        y_copy(i, t, index).start()
        kept[i, t, index] = grads[i, t, index, core, half] + cr[i, t, index, half]

    ready, batch = [], []

    def error_chunk(t, index, slots):
        partial(0, t, index, slots, act[...], et)
        dact[...] += lax.dot_general(
            stack(dec_t, t, slots), stack(et, t, slots), (((0,), (0,)), ((), ())), preferred_element_type=F32
        )
        batch.append((t, index))

    def between(k):
        for t, index in ready:
            exchange(0, t, index)
        ready[:] = batch
        batch.clear()

    spread(sq_z, z, 0, tile, [{"lat": slot_id(x, y, z + k)} for k in range(1, NZ)])
    dact[...] = jnp.zeros(dact.shape, F32)
    gather(et, ag2_send, ag2_recv, error_chunk, between)
    tile = collect(sq_z, 0, NZ)
    spread(sq_x, x, 1, tile, [{"lat": slot_id(x + k, y, z)} for k in range(1, NX)])
    dpre = (dact[...] * pos2[...]).astype(BF16)

    trees = [Tree(t) for t in range(2)]
    for t in range(2):

        def step(index, carry):
            slots = [index * GROUP + k if t else index + NZ * k for k in range(GROUP)]
            partial(1, t, index, slots, dpre, xt)
            return carry

        lax.fori_loop(0, 8, step, 0)
        if t == 0:
            between(4)
    for t in range(2):

        def step(index, carry):
            exchange(1, t, index)
            return carry

        lax.fori_loop(0, 8, step, 0)

    keeps = [pltpu.make_async_copy(kept.at[i], own_out.at[i], keep_sem.at[i]) for i in range(2)]
    for keep in keeps:
        keep.start()
    tile = collect(sq_x, 1, NX)
    peers = [{"lat": slot_id(x, y + k // 4, z), "dp": lax.rem(dp + k, 4)} for k in range(1, 8)]
    spread(sq_y, y * 4 + dp, 2, tile, peers)
    tile = collect(sq_y, 2, 8)
    mse_ref[...] = jnp.broadcast_to(jnp.sum(tile, keepdims=True), mse_ref.shape)
    for i in range(2):
        for t in range(2):

            def step(index, carry):
                core_copy(i, t, index).wait_send()
                y_copy(i, t, index).wait()
                return carry

            lax.fori_loop(0, 8, step, 0)
    for keep in keeps:
        keep.wait()


def finish(own_ref, far_ref, err_ref, mse_ref, gd_ref, ge_ref, err_out, mse_out):
    tall = own_ref.shape[-1] // GROUP
    for i, out in enumerate((gd_ref, ge_ref)):
        sums = [[own_ref[i, t, k] + far_ref[i, t, k].astype(F32) for k in range(8)] for t in range(2)]
        for s in range(0, NSLOT, 2):
            pieces = []
            for n in (s, s + 1):
                xy, z = divmod(n, NZ)
                pieces.append(sums[0][z][:, xy * tall : (xy + 1) * tall])
                pieces.append(sums[1][xy][:, z * tall : (z + 1) * tall])
            out[:, s * 2 * tall : (s + 2) * 2 * tall] = jnp.concatenate(pieces, axis=1)
    err_out[...] = err_ref[...]
    mse_out[0, 0] = mse_ref[0, 0]


def local(inputs, dec_bias, enc_weight, enc_bias, dec_weight, other_recon, active_blocks):
    rows, width = inputs.shape
    tall = width // 2
    lats, features = dec_weight.shape
    share = lats // 4
    halves = (2, NSLOT, tall, rows)
    vmem = pl.BlockSpec(memory_space=pltpu.VMEM)
    hbm = pl.BlockSpec(memory_space=pl.ANY)
    dma = pltpu.SemaphoreType.DMA
    grad = (2, 2, 8, share, GROUP * tall)

    def coded(n):
        return pltpu.VMEM((2, n, tall, rows), jnp.int16), pltpu.VMEM((2, n, 1, 128), F32)

    error, mse, own, far = pl.pallas_call(
        kernel,
        name="sae_step",
        out_shape=(
            jax.ShapeDtypeStruct((width, rows), F32),
            jax.ShapeDtypeStruct((8, 128), F32),
            jax.ShapeDtypeStruct(grad, F32),
            jax.ShapeDtypeStruct(grad, BF16),
        ),
        in_specs=[vmem, vmem, hbm, vmem, hbm, vmem, vmem],
        out_specs=(vmem, vmem, hbm, hbm),
        scratch_shapes=[
            pltpu.VMEM((2, NSLOT, tall, lats), BF16),
            pltpu.VMEM(dec_weight.shape, BF16),
            pltpu.VMEM((2, NSLOT, tall, lats), BF16),
            pltpu.VMEM(halves, BF16),
            pltpu.VMEM(halves, BF16),
            pltpu.VMEM(halves, F32),
            *coded(NSLOT),
            *coded(NSLOT),
            *coded(2 * NZ),
            *coded(NZ),
            *coded(NZ),
            *coded(1),
            pltpu.VMEM((lats, rows), F32),
            pltpu.VMEM((lats, rows), BF16),
            pltpu.VMEM((lats, rows), F32),
            pltpu.VMEM((lats, rows), F32),
            pltpu.VMEM((2, 2, 8, 2, 2, share, GROUP * tall), F32),
            pltpu.VMEM((2, 2, 8, 2, share, GROUP * tall), F32),
            pltpu.VMEM(grad, BF16),
            pltpu.VMEM(grad, F32),
            pltpu.VMEM((NZ, 8, 128), F32),
            pltpu.VMEM((NX, 8, 128), F32),
            pltpu.VMEM((8, 8, 128), F32),
            pltpu.VMEM((3, 8, 128), F32),
            dma((3,)),
            dma((2,)),
            dma((2, NSLOT)),
            dma((2, 2)),
            dma((2, 2, NSLOT)),
            dma((2, 2, 2 * NZ)),
            dma((2, 2, NZ)),
            dma((2, 2, NZ)),
            dma((2, 2, 1)),
            dma((2,)),
            dma((2, NSLOT)),
            dma((2, 2, 8)),
            dma((2, 2, 8)),
            dma((2, 2, 8)),
            dma((2, 2, 8)),
            dma((2,)),
            dma((3,)),
            dma((3,)),
        ],
        compiler_params=pltpu.CompilerParams(
            collective_id=0, has_side_effects=True, vmem_limit_bytes=60 * 2**20
        ),
    )(
        inputs.T,
        dec_bias.reshape(1, -1),
        enc_weight.reshape(NSLOT, 2, tall, lats),
        enc_bias.reshape(1, -1),
        dec_weight,
        other_recon.T,
        active_blocks.T,
    )
    cut = 16
    part_spec = pl.BlockSpec((2, 2, 8, cut, GROUP * tall), lambda g: (0, 0, 0, g, 0))
    out_spec = pl.BlockSpec((cut, features), lambda g: (g, 0))
    err_spec = pl.BlockSpec((cut, rows), lambda g: (g, 0))
    scalar = pl.BlockSpec(memory_space=pltpu.SMEM)
    grad_dec, grad_enc, error, mse = pl.pallas_call(
        finish,
        name="finish",
        grid=(share // cut,),
        out_shape=(
            jax.ShapeDtypeStruct((share, features), F32),
            jax.ShapeDtypeStruct((share, features), F32),
            jax.ShapeDtypeStruct((width, rows), F32),
            jax.ShapeDtypeStruct((1, 1), F32),
        ),
        in_specs=[part_spec, part_spec, err_spec, scalar],
        out_specs=(out_spec, out_spec, err_spec, scalar),
    )(own, far, error, mse)
    return error.T, mse.reshape(()), grad_dec, grad_enc.T


def solution(mesh):
    placed = (
        P("dp", "lat"),
        P("lat"),
        P(None, "lat"),
        P("lat"),
        P("lat", None),
        P("dp", "lat"),
        P("dp", "lat"),
    )
    return jax.shard_map(
        local,
        mesh=mesh,
        in_specs=placed,
        out_specs=(P("dp", "lat"), P(), P(("lat", "dp"), None), P(None, ("lat", "dp"))),
        check_vma=False,
    )
```

```python
import functools

import jax
import jax.numpy as jnp
from jax import lax
from jax.experimental import pallas as pl
from jax.experimental.pallas import tpu as pltpu
from jax.sharding import PartitionSpec as P

MESH = pl.DeviceIdType.MESH
NX, NY, NZ = 4, 2, 8
NSLOT = NX * NY * NZ
GROUP = 8
BF16, F32 = jnp.bfloat16, jnp.float32


def place():
    lat = lax.axis_index("lat")
    return lax.div(lat, NY * NZ), lax.rem(lax.div(lat, NZ), NY), lax.rem(lat, NZ)


def slot_id(x, y, z):
    return (lax.rem(x + 2 * NX, NX) * NY + lax.rem(y + 2, NY)) * NZ + lax.rem(z + 2 * NZ, NZ)


def offset(k):
    half = lax.div(k + 1, 2)
    return jnp.where(lax.rem(k, 2) == 1, -half, half)


class Tree:
    def __init__(self, t):
        self.t = t
        self.na, self.nb = (NZ, NX) if t else (NX, NZ)
        self.x, self.y, self.z = place()

    def sid(self, a, b, j):
        if self.t:
            return slot_id(self.x + b, self.y + j, self.z + a)
        return slot_id(self.x + a, self.y + j, self.z + b)

    def parity(self, j):
        return lax.rem(self.y + j, 2)

    def row(self, a):
        n = self.na
        return lax.rem((self.z if self.t else self.x) + a + 2 * n, n)

    def column(self, a, j):
        return self.row(a) * 2 + self.parity(j)

    def chunks(self, b):
        if self.t:
            base = lax.rem(self.x + b + 2 * NX, NX) * NY
            return [(base + i, [(base + i) * GROUP + k for k in range(GROUP)]) for i in range(NY)]
        base = lax.rem(self.z + b + 2 * NZ, NZ)
        return [(base, [base + NZ * k for k in range(GROUP)])]


def wait_for(ref, sem):
    pltpu.make_async_copy(ref, ref, sem).wait()


def each(n, *bodies):
    def step(c, carry):
        for body in bodies:
            body(c)
        return carry

    lax.fori_loop(0, n, step, 0)


class Gather:
    def __init__(self, t, buf, send_sem, recv_sem):
        self.tree = Tree(t)
        self.buf, self.send_sem, self.recv_sem = buf.at[t], send_sem.at[t], recv_sem.at[t]

    def send(self, s, a=0, b=0, j=0):
        pltpu.make_async_remote_copy(
            src_ref=self.buf.at[s],
            dst_ref=self.buf.at[s],
            send_sem=self.send_sem,
            recv_sem=self.recv_sem.at[s],
            device_id={"lat": self.tree.sid(a, b, j)},
            device_id_type=MESH,
        ).start()

    def wait(self, s):
        wait_for(self.buf.at[s], self.recv_sem.at[s])

    def onward(self, s):
        self.send(s, b=1)
        self.send(s, b=-1)

    def own(self):
        s = self.tree.sid(0, 0, 0)
        self.send(s, a=1)
        self.send(s, a=-1)
        self.send(s, j=1)
        self.onward(s)

    def from_y(self, a):
        s = self.tree.sid(a, 0, 1)
        self.wait(s)
        self.onward(s)

    def ring_a(self, h):
        t = self.tree
        far = t.na // 2
        for d in (-1, 1) if h < far else (1,):
            s = t.sid(d * h, 0, 0)
            self.wait(s)
            if h + 1 < far:
                self.send(s, a=-d)
            elif h < far:
                pl.when(t.y == (d + 1) // 2)(functools.partial(self.send, s, a=-d))
            self.send(s, j=1)
            self.onward(s)
        self.from_y(1 - h)
        if h > 1:
            self.from_y(h - 1)
        if h == far:
            self.from_y(h)

    def ring_b(self, h, c):
        t = self.tree
        far = t.nb // 2
        a, j = offset(lax.div(c, 2)), lax.rem(c, 2)
        if h == far:
            self.wait(t.sid(a, h, j))
            return
        for d in (-1, 1):
            s = t.sid(a, d * h, j)
            self.wait(s)
            if h + 1 < far:
                self.send(s, b=-d)
            else:
                pl.when(t.parity(j) == (d + 1) // 2)(functools.partial(self.send, s, b=-d))

    def end(self):
        wait_for(self.buf.at[pl.ds(0, NSLOT - 1)], self.send_sem)


def gather(buf, send_sem, recv_sem, eat, idle):
    p, q = (Gather(t, buf, send_sem, recv_sem) for t in range(2))

    def eat_all(g, *offsets):
        for b in offsets:
            for index, slots in g.tree.chunks(b):
                eat(g.tree.t, index, slots)

    p.own()
    q.own()
    p.ring_a(1)
    q.ring_a(1)
    p.ring_a(2)
    q.ring_a(2)
    q.ring_a(3)
    each(8, lambda c: p.ring_b(1, c))
    q.ring_a(4)
    idle(0)
    eat_all(p, 0)
    each(8, lambda c: p.ring_b(2, c), lambda c: q.ring_b(1, c))
    eat_all(p, -1, 1)
    eat_all(q, 0)
    idle(1)
    each(8, lambda c: p.ring_b(3, c), lambda c: q.ring_b(1, c + 8))
    eat_all(p, -2, 2)
    eat_all(q, -1, 1)
    idle(2)
    each(8, lambda c: p.ring_b(4, c), lambda c: q.ring_b(2, c))
    each(8, lambda c: q.ring_b(2, c + 8))
    eat_all(p, -3, 3, 4)
    eat_all(q, 2)
    idle(3)
    p.end()
    q.end()


def tiled(row, shape):
    return jnp.broadcast_to(jnp.concatenate([row] * (shape[1] // 128), axis=1), shape)


LEVELS = 32000.0


def encode(v):
    size = jnp.abs(v)
    top = functools.reduce(jnp.maximum, [size[:, i : i + 128] for i in range(0, v.shape[1], 128)])
    top = jnp.maximum(jnp.max(top, axis=0, keepdims=True), 1e-30)
    return jnp.round(v * tiled(LEVELS / top, v.shape)).astype(jnp.int16), top * (1.0 / LEVELS)


def decode(q, scale):
    return q.astype(F32) * tiled(scale, q.shape)


class Scatter:
    def __init__(self, t, part, out, r1, r2, y1, a1, a2, send_sem, r1_sem, r2_sem, y1_sem, a1_sem, a2_sem):
        self.tree = Tree(t)
        self.part = part.at[t]
        self.out, self.send_sem = [o.at[t] for o in out], [send_sem.at[t, i] for i in range(2)]
        bufs = {"r1": (r1, r1_sem), "r2": (r2, r2_sem), "y1": (y1, y1_sem), "a1": (a1, a1_sem), "a2": (a2, a2_sem)}
        self.bufs = {
            name: ([r.at[t] for r in refs], [sem.at[t, i] for i in range(2)]) for name, (refs, sem) in bufs.items()
        }

    def send(self, s, name, k, a=0, b=0, j=0):
        self.out[0][s], self.out[1][s] = encode(self.part[s])
        refs, sems = self.bufs[name]
        for i in range(2):
            pltpu.make_async_remote_copy(
                src_ref=self.out[i].at[s],
                dst_ref=refs[i].at[k],
                send_sem=self.send_sem[i],
                recv_sem=sems[i].at[k],
                device_id={"lat": self.tree.sid(a, b, j)},
                device_id_type=MESH,
            ).start()

    def take(self, s, name, k):
        refs, sems = self.bufs[name]
        for i in range(2):
            wait_for(refs[i].at[k], sems[i].at[k])
        self.part[s] += decode(refs[0][k], refs[1][k])

    def col(self, c):
        return offset(self.tree.na - 1 - lax.div(c, 2)), 1 - lax.rem(c, 2)

    def first(self, c):
        t = self.tree
        a, j = self.col(c)
        s = t.sid(a, t.nb // 2, j)
        for d in (-1, 1):
            pl.when(t.parity(j) == (d + 1) // 2)(functools.partial(self.send, s, "r1", s, b=d))

    def hop(self, h, c):
        t = self.tree
        a, j = self.col(c)
        for d in (-1, 1):
            s = t.sid(a, d * h, j)
            if h == t.nb // 2 - 1:
                pl.when(t.parity(j) == (d + 1) // 2)(functools.partial(self.take, s, "r1", s))
            else:
                self.take(s, "r1", s)
            if h == 1 and d == 1:
                self.send(s, "r2", t.column(a, j), b=d)
            else:
                self.send(s, "r1", s, b=d)

    def own_b(self, a, j):
        s = self.tree.sid(a, 0, j)
        self.take(s, "r1", s)
        self.take(s, "r2", self.tree.column(a, j))
        return s

    def to_y(self, *offsets):
        for a in offsets:
            self.send(self.own_b(a, 1), "y1", self.tree.row(a), j=1)

    def with_y(self, a):
        s, k = self.own_b(a, 0), self.tree.row(a)
        self.take(s, "y1", k)
        return s, k

    def ring_a(self, h):
        t = self.tree
        far = t.na // 2
        if h == far:
            s, k = self.with_y(h)
            for d in (-1, 1):
                pl.when(t.y == (d + 1) // 2)(functools.partial(self.send, s, "a1", k, a=d))
            return
        if h == 0:
            s, k = self.with_y(0)
            self.take(s, "a1", k)
            self.take(s, "a2", 0)
            return
        for d in (-1, 1):
            s, k = self.with_y(d * h)
            if h == far - 1:
                pl.when(t.y == (d + 1) // 2)(functools.partial(self.take, s, "a1", k))
            else:
                self.take(s, "a1", k)
            if h == 1 and d == 1:
                self.send(s, "a2", 0, a=d)
            else:
                self.send(s, "a1", k, a=d)

    def end(self):
        for i in range(2):
            wait_for(self.out[i].at[pl.ds(0, NSLOT - 1)], self.send_sem[i])


def scatter(make, *refs):
    p, q = (Scatter(t, *refs) for t in range(2))

    def make_all(g, *offsets):
        for b in offsets:
            for _, slots in g.tree.chunks(b):
                make(g.tree.t, slots)

    make_all(q, 2)
    make_all(p, 4)
    each(8, q.first, lambda c: q.first(c + 8), p.first)
    make_all(q, -1, 1)
    make_all(p, -3, 3)
    each(8, lambda c: q.hop(1, c), lambda c: p.hop(3, c))
    make_all(p, -2, 2)
    each(8, lambda c: q.hop(1, c + 8), lambda c: p.hop(2, c))
    make_all(q, 0)
    make_all(p, -1, 1, 0)
    q.to_y(4, -3, 3)
    each(4, lambda c: p.hop(1, c))
    q.ring_a(4)
    q.to_y(-2, 2)
    each(4, lambda c: p.hop(1, c + 4))
    q.ring_a(3)
    q.to_y(-1, 1)
    p.to_y(2, -1, 1)
    q.ring_a(2)
    q.to_y(0)
    p.ring_a(2)
    q.ring_a(1)
    p.to_y(0)
    p.ring_a(1)
    q.ring_a(0)
    p.ring_a(0)
    p.end()
    q.end()


def column_of(row):
    n = row.shape[1]
    eye = lax.broadcasted_iota(jnp.int32, (n, n), 0) == lax.broadcasted_iota(jnp.int32, (n, n), 1)
    return jnp.sum(jnp.where(eye, jnp.broadcast_to(row, (n, n)), 0.0), axis=1, keepdims=True)


def kernel(
    x_ref, bias_ref, enc_hbm, ebias_ref, dec_hbm, other_ref, gate_ref,
    err_ref, mse_ref, own_out, far_out,
    enc, dec, dec_t, xt, et, part, out_q, out_s, r1_q, r1_s, r2_q, r2_s, y1_q, y1_s, a1_q, a1_s, a2_q, a2_s,
    pre, act, pos2, dact, grads, cr, ys, kept, sq_z, sq_x, sq_y, sq_t,
    load_sem, ag_send, ag_recv, rs_send, r1_sem, r2_sem, y1_sem, a1_sem, a2_sem,
    ag2_send, ag2_recv, core_send, core_recv, yx_send, yx_recv, keep_sem, sq_send, sq_recv,
):
    x, y, z = place()
    dp = lax.axis_index("dp")
    core, half = lax.rem(dp, 2), lax.div(dp, 2)
    own = slot_id(x, y, z)
    width, rows = x_ref.shape
    tall = width // 2
    lats = dec.shape[0]
    block = lats // gate_ref.shape[0]

    loads = [pltpu.make_async_copy(enc_hbm.at[:, t], enc.at[t], load_sem.at[t]) for t in range(2)]
    loads.append(pltpu.make_async_copy(dec_hbm, dec, load_sem.at[2]))
    for load in loads:
        load.start()

    barrier = pltpu.get_barrier_semaphore()
    for k in range(1, NX):
        pl.semaphore_signal(barrier, inc=1, device_id={"lat": slot_id(x + k, y, z)}, device_id_type=MESH)
    for k in range(1, NZ):
        pl.semaphore_signal(barrier, inc=1, device_id={"lat": slot_id(x, y, z + k)}, device_id_type=MESH)
    for k in range(1, 8):
        pl.semaphore_signal(
            barrier,
            inc=1,
            device_id={"lat": slot_id(x, y + k // 4, z), "dp": lax.rem(dp + k, 4)},
            device_id_type=MESH,
        )
    bias_col = column_of(bias_ref[...].astype(F32))
    x_f = x_ref[...].astype(F32)
    centered = (x_f - bias_col).astype(BF16)
    for t in range(2):
        xt[t, own] = centered[t * tall : (t + 1) * tall]
    pl.semaphore_wait(barrier, NX - 1 + NZ - 1 + 7)

    def stack(ref, t, slots):
        return jnp.concatenate([ref[t, s] for s in slots], axis=0)

    def encode_chunk(t, index, slots):
        pre[...] += lax.dot_general(
            stack(enc, t, slots), stack(xt, t, slots), (((0,), (0,)), ((), ())), preferred_element_type=F32
        )

    def turn(k):
        if k == 0:
            for load in loads:
                load.wait()
            pre[...] = jnp.broadcast_to(column_of(ebias_ref[...]), pre.shape)
        if k == 1:
            for i in range(NSLOT // 2):
                both = dec[:, 2 * i * width : 2 * (i + 1) * width].T
                for n in range(4):
                    dec_t[n % 2, 2 * i + n // 2] = both[n * tall : (n + 1) * tall]

    gather(xt, ag_send, ag_recv, encode_chunk, turn)

    positive = jnp.maximum(pre[...], 0.0)
    gate = jnp.concatenate(
        [jnp.broadcast_to(gate_ref[i : i + 1, :].astype(F32), (block, rows)) for i in range(lats // block)], axis=0
    )
    gated = positive * gate
    act[...] = (positive * gated).astype(BF16)
    pos2[...] = 2.0 * gated

    def decode_chunk(t, slots):
        out = jnp.dot(stack(dec_t, t, slots), act[...], preferred_element_type=F32)
        for i, s in enumerate(slots):
            part[t, s] = out[i * tall : (i + 1) * tall]

    scatter(
        decode_chunk, part, (out_q, out_s), (r1_q, r1_s), (r2_q, r2_s), (y1_q, y1_s), (a1_q, a1_s), (a2_q, a2_s),
        rs_send, r1_sem, r2_sem, y1_sem, a1_sem, a2_sem,
    )

    total = jnp.concatenate([part[t, own] for t in range(2)], axis=0)
    error = total + other_ref[...] + bias_col - x_f
    err_ref[...] = error
    for t in range(2):
        et[t, own] = error[t * tall : (t + 1) * tall].astype(BF16)
    sq = error * error
    tile = sum(sq[8 * i : 8 * i + 8] for i in range(width // 8))
    tile = sum(tile[:, 128 * i : 128 * i + 128] for i in range(rows // 128))
    tile = tile * (1.0 / (rows * 4 * width * NSLOT))

    def spread(dst, mine, level, value, peers):
        dst[mine] = value
        sq_t[level] = value
        for dev in peers:
            pltpu.make_async_remote_copy(
                src_ref=sq_t.at[level],
                dst_ref=dst.at[mine],
                send_sem=sq_send.at[level],
                recv_sem=sq_recv.at[level],
                device_id=dev,
                device_id_type=MESH,
            ).start()

    def collect(dst, level, n):
        view = dst.at[pl.ds(0, n - 1)]
        wait_for(view, sq_recv.at[level])
        wait_for(view, sq_send.at[level])
        return sum(dst[i] for i in range(n))

    share = lats // 4
    other_core = lax.rem(core + 1, 2)

    def core_copy(i, t, index):
        return pltpu.make_async_remote_copy(
            src_ref=grads.at[i, t, index, other_core],
            dst_ref=cr.at[i, t, index],
            send_sem=core_send.at[i, t, index],
            recv_sem=core_recv.at[i, t, index],
            device_id={"dp": half * 2 + other_core},
            device_id_type=MESH,
        )

    def y_copy(i, t, index):
        return pltpu.make_async_remote_copy(
            src_ref=ys.at[i, t, index],
            dst_ref=far_out.at[i, t, index],
            send_sem=yx_send.at[i, t, index],
            recv_sem=yx_recv.at[i, t, index],
            device_id={"dp": (1 - half) * 2 + core},
            device_id_type=MESH,
        )

    def partial(i, t, index, slots, lhs, ref):
        out = lax.dot_general(lhs, stack(ref, t, slots), (((1,), (1,)), ((), ())), preferred_element_type=F32)
        for h in range(2):
            for c in range(2):
                n = h * 2 + c
                grads[i, t, index, c, h] = out[n * share : (n + 1) * share]
        core_copy(i, t, index).start()

    def exchange(i, t, index):
        core_copy(i, t, index).wait_recv()
        ys[i, t, index] = (grads[i, t, index, core, 1 - half] + cr[i, t, index, 1 - half]).astype(BF16)
        y_copy(i, t, index).start()
        kept[i, t, index] = grads[i, t, index, core, half] + cr[i, t, index, half]

    ready, batch = [], []

    def error_chunk(t, index, slots):
        partial(0, t, index, slots, act[...], et)
        dact[...] += lax.dot_general(
            stack(dec_t, t, slots), stack(et, t, slots), (((0,), (0,)), ((), ())), preferred_element_type=F32
        )
        batch.append((t, index))

    def between(k):
        for t, index in ready:
            exchange(0, t, index)
        ready[:] = batch
        batch.clear()

    spread(sq_z, z, 0, tile, [{"lat": slot_id(x, y, z + k)} for k in range(1, NZ)])
    dact[...] = jnp.zeros(dact.shape, F32)
    gather(et, ag2_send, ag2_recv, error_chunk, between)
    tile = collect(sq_z, 0, NZ)
    spread(sq_x, x, 1, tile, [{"lat": slot_id(x + k, y, z)} for k in range(1, NX)])
    dpre = (dact[...] * pos2[...]).astype(BF16)

    trees = [Tree(t) for t in range(2)]
    for t in range(2):

        def step(index, carry):
            slots = [index * GROUP + k if t else index + NZ * k for k in range(GROUP)]
            partial(1, t, index, slots, dpre, xt)
            return carry

        lax.fori_loop(0, 8, step, 0)
        if t == 0:
            between(4)
    for t in range(2):

        def step(index, carry):
            exchange(1, t, index)
            return carry

        lax.fori_loop(0, 8, step, 0)

    keeps = [pltpu.make_async_copy(kept.at[i], own_out.at[i], keep_sem.at[i]) for i in range(2)]
    for keep in keeps:
        keep.start()
    tile = collect(sq_x, 1, NX)
    peers = [{"lat": slot_id(x, y + k // 4, z), "dp": lax.rem(dp + k, 4)} for k in range(1, 8)]
    spread(sq_y, y * 4 + dp, 2, tile, peers)
    tile = collect(sq_y, 2, 8)
    mse_ref[...] = jnp.broadcast_to(jnp.sum(tile, keepdims=True), mse_ref.shape)
    for i in range(2):
        for t in range(2):

            def step(index, carry):
                core_copy(i, t, index).wait_send()
                y_copy(i, t, index).wait()
                return carry

            lax.fori_loop(0, 8, step, 0)
    for keep in keeps:
        keep.wait()


def finish(own_ref, far_ref, err_ref, mse_ref, gd_ref, ge_ref, err_out, mse_out):
    tall = own_ref.shape[-1] // GROUP
    for i, out in enumerate((gd_ref, ge_ref)):
        sums = [[own_ref[i, t, k] + far_ref[i, t, k].astype(F32) for k in range(8)] for t in range(2)]
        for s in range(0, NSLOT, 2):
            pieces = []
            for n in (s, s + 1):
                xy, z = divmod(n, NZ)
                pieces.append(sums[0][z][:, xy * tall : (xy + 1) * tall])
                pieces.append(sums[1][xy][:, z * tall : (z + 1) * tall])
            out[:, s * 2 * tall : (s + 2) * 2 * tall] = jnp.concatenate(pieces, axis=1)
    err_out[...] = err_ref[...]
    mse_out[0, 0] = mse_ref[0, 0]


def local(inputs, dec_bias, enc_weight, enc_bias, dec_weight, other_recon, active_blocks):
    rows, width = inputs.shape
    tall = width // 2
    lats, features = dec_weight.shape
    share = lats // 4
    halves = (2, NSLOT, tall, rows)
    vmem = pl.BlockSpec(memory_space=pltpu.VMEM)
    hbm = pl.BlockSpec(memory_space=pl.ANY)
    dma = pltpu.SemaphoreType.DMA
    grad = (2, 2, 8, share, GROUP * tall)

    def coded(n):
        return pltpu.VMEM((2, n, tall, rows), jnp.int16), pltpu.VMEM((2, n, 1, 128), F32)

    error, mse, own, far = pl.pallas_call(
        kernel,
        name="sae_step",
        out_shape=(
            jax.ShapeDtypeStruct((width, rows), F32),
            jax.ShapeDtypeStruct((8, 128), F32),
            jax.ShapeDtypeStruct(grad, F32),
            jax.ShapeDtypeStruct(grad, BF16),
        ),
        in_specs=[vmem, vmem, hbm, vmem, hbm, vmem, vmem],
        out_specs=(vmem, vmem, hbm, hbm),
        scratch_shapes=[
            pltpu.VMEM((2, NSLOT, tall, lats), BF16),
            pltpu.VMEM(dec_weight.shape, BF16),
            pltpu.VMEM((2, NSLOT, tall, lats), BF16),
            pltpu.VMEM(halves, BF16),
            pltpu.VMEM(halves, BF16),
            pltpu.VMEM(halves, F32),
            *coded(NSLOT),
            *coded(NSLOT),
            *coded(2 * NZ),
            *coded(NZ),
            *coded(NZ),
            *coded(1),
            pltpu.VMEM((lats, rows), F32),
            pltpu.VMEM((lats, rows), BF16),
            pltpu.VMEM((lats, rows), F32),
            pltpu.VMEM((lats, rows), F32),
            pltpu.VMEM((2, 2, 8, 2, 2, share, GROUP * tall), F32),
            pltpu.VMEM((2, 2, 8, 2, share, GROUP * tall), F32),
            pltpu.VMEM(grad, BF16),
            pltpu.VMEM(grad, F32),
            pltpu.VMEM((NZ, 8, 128), F32),
            pltpu.VMEM((NX, 8, 128), F32),
            pltpu.VMEM((8, 8, 128), F32),
            pltpu.VMEM((3, 8, 128), F32),
            dma((3,)),
            dma((2,)),
            dma((2, NSLOT)),
            dma((2, 2)),
            dma((2, 2, NSLOT)),
            dma((2, 2, 2 * NZ)),
            dma((2, 2, NZ)),
            dma((2, 2, NZ)),
            dma((2, 2, 1)),
            dma((2,)),
            dma((2, NSLOT)),
            dma((2, 2, 8)),
            dma((2, 2, 8)),
            dma((2, 2, 8)),
            dma((2, 2, 8)),
            dma((2,)),
            dma((3,)),
            dma((3,)),
        ],
        compiler_params=pltpu.CompilerParams(
            collective_id=0, has_side_effects=True, vmem_limit_bytes=60 * 2**20
        ),
    )(
        inputs.T,
        dec_bias.reshape(1, -1),
        enc_weight.reshape(NSLOT, 2, tall, lats),
        enc_bias.reshape(1, -1),
        dec_weight,
        other_recon.T,
        active_blocks.T,
    )
    cut = 32
    part_spec = pl.BlockSpec((2, 2, 8, cut, GROUP * tall), lambda g: (0, 0, 0, g, 0))
    out_spec = pl.BlockSpec((cut, features), lambda g: (g, 0))
    err_spec = pl.BlockSpec((cut, rows), lambda g: (g, 0))
    scalar = pl.BlockSpec(memory_space=pltpu.SMEM)
    grad_dec, grad_enc, error, mse = pl.pallas_call(
        finish,
        name="finish",
        grid=(share // cut,),
        out_shape=(
            jax.ShapeDtypeStruct((share, features), F32),
            jax.ShapeDtypeStruct((share, features), F32),
            jax.ShapeDtypeStruct((width, rows), F32),
            jax.ShapeDtypeStruct((1, 1), F32),
        ),
        in_specs=[part_spec, part_spec, err_spec, scalar],
        out_specs=(out_spec, out_spec, err_spec, scalar),
    )(own, far, error, mse)
    return error.T, mse.reshape(()), grad_dec, grad_enc.T


def solution(mesh):
    placed = (
        P("dp", "lat"),
        P("lat"),
        P(None, "lat"),
        P("lat"),
        P("lat", None),
        P("dp", "lat"),
        P("dp", "lat"),
    )
    return jax.shard_map(
        local,
        mesh=mesh,
        in_specs=placed,
        out_specs=(P("dp", "lat"), P(), P(("lat", "dp"), None), P(None, ("lat", "dp"))),
        check_vma=False,
    )
```
